32 devices in a mesh: shard: 16 (over z, x, core), rep: 2 (over y).
Axes of the slice: x: 2, y: 2, z: 4, core: 2. Of those that a mesh axis runs over, the one named last changes fastest.
Arguments:
- images: bfloat16 [64, 197, 768], P(('shard', 'rep')), may hold values from -6 to 6
- image_counts: int32 [32], P(('shard', 'rep')), may hold values from 1 to 2, as said below
- qkv_weight: bfloat16 [768, 2304], P('shard'), may hold values from -0.21875 to 0.21875
- qv_bias: bfloat16 [2, 768], P(None, 'shard'), may hold values from -3 to 3
- out_weight: bfloat16 [768, 768], P('shard'), may hold values from -1.75 to 1.75
- out_bias: bfloat16 [768], P('shard'), may hold values from -3 to 3
- up_weight: bfloat16 [768, 3072], P('shard'), may hold values from -0.21875 to 0.21875
- up_bias: bfloat16 [3072], P('shard'), may hold values from -3 to 3
- down_weight: bfloat16 [3072, 768], P('shard'), may hold values from -0.109375 to 0.109375
- down_bias: bfloat16 [768], P('shard'), may hold values from -3 to 3
- norm1_gain: bfloat16 [768], P('shard'), may hold values from 0.099609375 to 1.8984375
- norm1_shift: bfloat16 [768], P('shard'), may hold values from -3 to 3
- norm2_gain: bfloat16 [768], P('shard'), may hold values from 0.099609375 to 1.8984375
- norm2_shift: bfloat16 [768], P('shard'), may hold values from -3 to 3
- cotangent: bfloat16 [64, 197, 768], P(('shard', 'rep')), may hold values from -6 to 6
Outputs:
- encoded: bfloat16 [64, 197, 768], P(('shard', 'rep'))
- input_grad: float32 [64, 197, 768], P(('shard', 'rep'))
- qkv_weight_grad: float32 [768, 2304], P('shard')
- qv_bias_grad: float32 [2, 768], P(None, 'shard')
- out_weight_grad: float32 [768, 768], P('shard')
- out_bias_grad: float32 [768], P('shard')
- up_weight_grad: float32 [768, 3072], P('shard')
- up_bias_grad: float32 [3072], P('shard')
- down_weight_grad: float32 [3072, 768], P('shard')
- down_bias_grad: float32 [768], P('shard')
- norm1_gain_grad: float32 [768], P('shard')
- norm1_shift_grad: float32 [768], P('shard')
- norm2_gain_grad: float32 [768], P('shard')
- norm2_shift_grad: float32 [768], P('shard')
The draws below stay inside these ranges and needn't reach their ends.
Inputs may be any that keep to these rules, and one draw needn't show every extreme that they name: Device d has live images in its first image_counts[d] of 2 slots, the others are padding; some device has 2 live images and some device one.
All inputs are finite; a program needn't handle non-finite values.
Results may differ from the reference program's by a relative error of at most 0.011.
Values may be sent and summed in bfloat16 or wider, within the bound.
A program may use at most 128 MiB of HBM per device.

```python
import jax
import jax.numpy as jnp
from jax import lax

D = 768
HEADS = 12
HEAD_DIM = 64
FF = 3072
SEQ = 197
IMG_DEV = 2
NDEV = 32
IMAGES = 64


def draw_image_counts(key, part):
    key_counts = jax.random.fold_in(key, 11)
    key_place = jax.random.fold_in(key, 23)
    counts = jax.random.randint(key_counts, (NDEV,), 1, IMG_DEV + 1)
    chosen = jax.random.randint(key_place, (), 0, NDEV)
    counts = counts.at[chosen].set(IMG_DEV)
    counts = counts.at[(chosen + 1) % NDEV].set(1)
    return counts.astype(jnp.int32)


def block_scale(key, dims, shards, smallest, high):
    loudness = 1.0
    for dim, shards_of in shards:
        steps = jax.random.uniform(jax.random.fold_in(jax.random.fold_in(key, 6), dim), (shards_of,), jnp.float32, smallest / len(shards), high / len(shards))
        loudness = loudness * jnp.repeat(jnp.exp(steps), dims[dim] // shards_of).reshape((-1,) + (1,) * (len(dims) - 1 - dim))
    return loudness


def bell_draw(rng, extent, spread, reach, split=(), dtype=jnp.bfloat16):
    values = jax.random.normal(rng, extent, jnp.float32) * spread
    if len(split) > 0:
        values = block_scale(rng, extent, split, -0.22, 0.18) * values
    return jnp.clip(values, min=-reach, max=reach).astype(dtype)


def setup_inputs(seed: int = 0) -> dict:
    keys = jax.random.split(jax.random.key(seed), 16)
    images = bell_draw(keys[0], (IMAGES, SEQ, D), 1.0, 6.0, ((0, 32),))
    image_counts = draw_image_counts(jax.random.fold_in(keys[15], 71), 0)
    qkv_weight = bell_draw(keys[2], (D, 3 * D), D ** -0.5, 0.21875, ((0, 16),))
    qv_bias = bell_draw(keys[3], (2, D), 0.5, 3.0, ((1, 16),))
    out_weight = bell_draw(keys[4], (D, D), (D // 64) ** -0.5, 1.75, ((0, 16),))
    out_bias = bell_draw(keys[5], (D,), 0.5, 3.0, ((0, 16),))
    up_weight = bell_draw(keys[6], (D, FF), D ** -0.5, 0.21875, ((0, 16),))
    up_bias = bell_draw(keys[7], (FF,), 0.5, 3.0, ((0, 16),))
    down_weight = bell_draw(keys[8], (FF, D), FF ** -0.5, 0.109375, ((0, 16),))
    down_bias = bell_draw(keys[9], (D,), 0.5, 3.0, ((0, 16),))
    norm1_gain = jnp.clip(1.0 + 0.18 * jax.random.normal(keys[10], (D,), jnp.float32), 0.099609375, 1.8984375).astype(jnp.bfloat16)
    norm1_shift = bell_draw(keys[11], (D,), 0.5, 3.0, ((0, 16),))
    norm2_gain = jnp.clip(1.0 + 0.18 * jax.random.normal(keys[12], (D,), jnp.float32), 0.099609375, 1.8984375).astype(jnp.bfloat16)
    norm2_shift = bell_draw(keys[13], (D,), 0.5, 3.0, ((0, 16),))
    cotangent = bell_draw(keys[14], (IMAGES, SEQ, D), 1.0, 6.0, ((0, 32),))
    return dict(images=images, image_counts=image_counts, qkv_weight=qkv_weight, qv_bias=qv_bias, out_weight=out_weight, out_bias=out_bias, up_weight=up_weight, up_bias=up_bias, down_weight=down_weight, down_bias=down_bias, norm1_gain=norm1_gain, norm1_shift=norm1_shift, norm2_gain=norm2_gain, norm2_shift=norm2_shift, cotangent=cotangent)


@jax.custom_vjp
def low(v):
    return lax.optimization_barrier(v.astype(jnp.bfloat16)).astype(jnp.float32)

@jax.custom_vjp
def low_back(v):
    return v

def low_keep(v):
    return (low(v), None)

def low_pass(kept, grad):
    return (grad,)

def back_keep(v):
    return (v, None)

def back_low(kept, grad):
    return (low(grad),)
low.defvjp(low_keep, low_pass)
low_back.defvjp(back_keep, back_low)
highest = lax.Precision.HIGHEST
norm_eps = 1e-06

def layer_norm(value, scales, shifts):
    average = lax.optimization_barrier(jnp.mean(value, axis=-1, keepdims=True))
    centred = value - average
    variance = lax.optimization_barrier(jnp.mean(centred * centred, axis=-1, keepdims=True))
    return centred * lax.rsqrt(variance + norm_eps) * scales + shifts

def layer_forward(inputs, params):
    qkv_weight, qv_bias, out_weight, out_bias, up_weight, up_bias, down_weight, down_bias, norm1_gain, norm1_shift, norm2_gain, norm2_shift = params
    batch_count, seq_length, model_width = inputs.shape
    normed_one = low(layer_norm(inputs, norm1_gain, norm1_shift))
    full_bias = jnp.concatenate([qv_bias[0], jnp.zeros_like(qv_bias[0]), qv_bias[1]])
    projected = jnp.einsum('bsd,de->bse', normed_one, qkv_weight, precision=highest) + full_bias
    projected = low_back(low(projected))
    projected = projected.reshape(batch_count, seq_length, 3, HEADS, HEAD_DIM)
    queries = projected[:, :, 0]
    keys_part = projected[:, :, 1]
    values = projected[:, :, 2]
    scores = jnp.einsum('bqhd,bkhd->bhqk', queries, keys_part, precision=highest) * HEAD_DIM ** (-0.5)
    scores = low_back(scores)
    probs = jax.nn.softmax(scores, axis=-1)
    probs_low = low(probs)
    attended = jnp.einsum('bhqk,bkhd->bqhd', probs_low, values, precision=highest)
    attended = low_back(low(attended.reshape(batch_count, seq_length, model_width)))
    branch = low_back(jnp.einsum('bsd,de->bse', attended, out_weight, precision=highest) + out_bias)
    hidden = inputs + branch
    normed_two = low(layer_norm(hidden, norm2_gain, norm2_shift))
    upward = low_back(jnp.einsum('bsd,df->bsf', normed_two, up_weight, precision=highest) + up_bias)
    active = low(jax.nn.gelu(upward, approximate=False))
    mlp_out = low_back(jnp.einsum('bsf,fd->bsd', active, down_weight, precision=highest) + down_bias)
    return hidden + mlp_out

def reference(images, image_counts, qkv_weight, qv_bias, out_weight, out_bias, up_weight, up_bias, down_weight, down_bias, norm1_gain, norm1_shift, norm2_gain, norm2_shift, cotangent):
    params = tuple((param.astype(jnp.float32) for param in (qkv_weight, qv_bias, out_weight, out_bias, up_weight, up_bias, down_weight, down_bias, norm1_gain, norm1_shift, norm2_gain, norm2_shift)))
    grouped_images = images.reshape(NDEV, IMG_DEV, SEQ, D)
    grouped_cot = cotangent.reshape(NDEV, IMG_DEV, SEQ, D)

    def one_device(totals, inputs):
        block, block_cot, live_count = inputs
        live_mask = (jnp.arange(IMG_DEV).astype(jnp.int32) < live_count).astype(jnp.float32)[:, None, None]
        result, pullback = jax.vjp(layer_forward, block.astype(jnp.float32), params)
        input_part, param_grads = pullback(block_cot.astype(jnp.float32) * live_mask)
        totals = jax.tree.map(lambda summed, addend: summed + addend, totals, param_grads)
        return (totals, ((result * live_mask).astype(jnp.bfloat16), input_part))
    initial = jax.tree.map(jnp.zeros_like, params)
    totals, (encoded, input_grad) = lax.scan(one_device, initial, (grouped_images, grouped_cot, image_counts))
    return (encoded.reshape(IMAGES, SEQ, D), input_grad.reshape(IMAGES, SEQ, D), totals[0], totals[1], totals[2], totals[3], totals[4], totals[5], totals[6], totals[7], totals[8], totals[9], totals[10], totals[11])
```

```python
import jax
import jax.numpy as jnp
from jax import lax
from jax.sharding import PartitionSpec as P

HEADS = 12
HEAD_DIM = 64


norm_eps = 1e-06


def normalize(value):
    average = jnp.mean(value, axis=-1, keepdims=True)
    centred = value - average
    variance = jnp.mean(centred * centred, axis=-1, keepdims=True)
    inverse = lax.rsqrt(variance + norm_eps)
    return (centred * inverse, inverse)


def norm_backward(grad_normed, unit_part, inverse, scales):
    grad_unit = grad_normed * scales
    mean_one = jnp.mean(grad_unit, axis=-1, keepdims=True)
    mean_two = jnp.mean(grad_unit * unit_part, axis=-1, keepdims=True)
    grad_input = inverse * (grad_unit - mean_one - unit_part * mean_two)
    return (grad_input, jnp.sum(grad_normed * unit_part, axis=0), jnp.sum(grad_normed, axis=0))


def exact_gelu(value):
    return jax.nn.gelu(value, approximate=False)


def bits_of(size):
    return size.bit_length() - 1


def swap(value, axis, bit):
    size = lax.axis_size(axis)
    return lax.ppermute(value, axis, [(i, i ^ (1 << bit)) for i in range(size)])


def halve(current, order):
    index = lax.axis_index("shard")
    remaining = list(range(bits_of(lax.axis_size("shard"))))[::-1]
    for bit in order:
        dim = remaining.index(bit)
        mine = (index >> bit) & 1
        sent = lax.dynamic_index_in_dim(current, 1 - mine, dim, keepdims=False)
        kept = lax.dynamic_index_in_dim(current, mine, dim, keepdims=False)
        came = swap(sent, "shard", bit)
        current = (kept.astype(jnp.float32) + came.astype(jnp.float32)).astype(current.dtype)
        remaining.remove(bit)
    return current


def replica_sum(current):
    bits = bits_of(lax.axis_size("rep"))
    for bit in range(bits):
        came = swap(current, "rep", bit)
        total = current.astype(jnp.float32) + came.astype(jnp.float32)
        current = total.astype(current.dtype) if bit < bits - 1 else total
    return current.astype(jnp.float32)


def owner_sum(grad, order):
    size = lax.axis_size("shard")
    rows, columns = grad.shape
    split = grad.reshape((2,) * bits_of(size) + (rows // size, columns))
    return replica_sum(halve(split, order))


def by_owner(vector):
    return vector.reshape(lax.axis_size("shard"), -1)


def shards(
    images,
    image_counts,
    qkv_weight,
    qv_bias,
    out_weight,
    out_bias,
    up_weight,
    up_bias,
    down_weight,
    down_bias,
    norm1_gain,
    norm1_shift,
    norm2_gain,
    norm2_shift,
    cotangent,
):
    f32 = jnp.float32
    bf16 = jnp.bfloat16
    batch_count, seq_length, model_width = images.shape
    token_count = batch_count * seq_length
    score_scale = HEAD_DIM ** (-0.5)
    size = lax.axis_size("shard")
    small_parts = [
        qv_bias.reshape(-1),
        out_bias,
        up_bias,
        down_bias,
        norm1_gain,
        norm1_shift,
        norm2_gain,
        norm2_shift,
    ]
    widths = [part.shape[0] for part in small_parts]
    small_width = sum(widths)
    padding = -small_width % 128
    small_own = jnp.concatenate(small_parts + [jnp.zeros((padding,), bf16)])[None]
    small_full = lax.all_gather(small_own, "shard", axis=0, tiled=True)
    pieces = []
    offset = 0
    for width in widths:
        pieces.append(small_full[:, offset : offset + width])
        offset += width
    full_qv_bias = pieces[0].reshape(size, 2, -1).transpose(1, 0, 2).reshape(2, -1)
    (
        full_out_bias,
        full_up_bias,
        full_down_bias,
        gain_one,
        shift_one,
        gain_two,
        shift_two,
    ) = [piece.reshape(-1) for piece in pieces[1:]]
    full_qkv = lax.all_gather(qkv_weight, "shard", axis=0, tiled=True)
    full_out = lax.all_gather(out_weight, "shard", axis=0, tiled=True)
    full_up = lax.all_gather(up_weight, "shard", axis=0, tiled=True)
    full_down = lax.all_gather(down_weight, "shard", axis=0, tiled=True)
    live_mask = (jnp.arange(batch_count) < image_counts[0]).astype(f32)[:, None]
    live_rows = jnp.repeat(live_mask, seq_length, axis=0)
    inputs = images.astype(f32).reshape(token_count, model_width)
    unit_one, inverse_one = normalize(inputs)
    normed_one = (unit_one * gain_one.astype(f32) + shift_one.astype(f32)).astype(bf16)
    bias_row = jnp.concatenate(
        [full_qv_bias[0], jnp.zeros_like(full_qv_bias[0]), full_qv_bias[1]]
    ).astype(f32)
    projected = (jnp.dot(normed_one, full_qkv, preferred_element_type=f32) + bias_row).astype(bf16)
    projected = projected.reshape(batch_count, seq_length, 3, HEADS, HEAD_DIM)
    queries = projected[:, :, 0]
    keys_part = projected[:, :, 1]
    values = projected[:, :, 2]
    scores = (
        jnp.einsum("bqhd,bkhd->bhqk", queries, keys_part, preferred_element_type=f32) * score_scale
    )
    probs = jax.nn.softmax(scores, axis=-1)
    probs_low = probs.astype(bf16)
    attended = jnp.einsum("bhqk,bkhd->bqhd", probs_low, values, preferred_element_type=f32)
    attended = attended.reshape(token_count, model_width).astype(bf16)
    branch = jnp.dot(attended, full_out, preferred_element_type=f32) + full_out_bias.astype(f32)
    hidden = inputs + branch
    unit_two, inverse_two = normalize(hidden)
    normed_two = (unit_two * gain_two.astype(f32) + shift_two.astype(f32)).astype(bf16)
    upward = jnp.dot(normed_two, full_up, preferred_element_type=f32) + full_up_bias.astype(f32)
    activation, gelu_pull = jax.vjp(exact_gelu, upward)
    active_low = activation.astype(bf16)
    mlp_out = jnp.dot(active_low, full_down, preferred_element_type=f32) + full_down_bias.astype(
        f32
    )
    encoded = (
        ((hidden + mlp_out) * live_rows).astype(bf16).reshape(batch_count, seq_length, model_width)
    )
    grad_output = cotangent.astype(f32).reshape(token_count, model_width) * live_rows
    grad_mlp = grad_output.astype(bf16)
    grad_down_bias = jnp.sum(grad_mlp.astype(f32), axis=0)
    grad_down = jnp.einsum("tf,td->fd", active_low, grad_mlp, preferred_element_type=f32).astype(bf16)
    grad_active = jnp.einsum("td,fd->tf", grad_mlp, full_down, preferred_element_type=f32)
    grad_upward = gelu_pull(grad_active)[0].astype(bf16)
    grad_up_bias = jnp.sum(grad_upward.astype(f32), axis=0)
    grad_up = jnp.einsum("td,tf->df", normed_two, grad_upward, preferred_element_type=f32).astype(bf16)
    grad_normed_two = jnp.einsum("tf,df->td", grad_upward, full_up, preferred_element_type=f32)
    grad_hidden_norm, grad_gain_two, grad_shift_two = norm_backward(
        grad_normed_two, unit_two, inverse_two, gain_two.astype(f32)
    )
    grad_hidden = grad_output + grad_hidden_norm
    grad_branch = grad_hidden.astype(bf16)
    grad_out_bias = jnp.sum(grad_branch.astype(f32), axis=0)
    grad_out = jnp.einsum("td,te->de", attended, grad_branch, preferred_element_type=f32).astype(bf16)
    grad_attended = jnp.einsum(
        "te,de->td", grad_branch, full_out, preferred_element_type=f32
    ).astype(bf16)
    grad_attended = grad_attended.reshape(batch_count, seq_length, HEADS, HEAD_DIM)
    grad_probs = jnp.einsum("bqhd,bkhd->bhqk", grad_attended, values, preferred_element_type=f32)
    grad_values = jnp.einsum(
        "bhqk,bqhd->bkhd", probs_low, grad_attended, preferred_element_type=f32
    )
    row_terms = jnp.sum(probs * grad_probs, axis=-1, keepdims=True)
    grad_scores = (probs * (grad_probs - row_terms)).astype(bf16)
    grad_queries = (
        jnp.einsum("bhqk,bkhd->bqhd", grad_scores, keys_part, preferred_element_type=f32)
        * score_scale
    )
    grad_keys = (
        jnp.einsum("bhqk,bqhd->bkhd", grad_scores, queries, preferred_element_type=f32)
        * score_scale
    )
    grad_projected = jnp.stack([grad_queries, grad_keys, grad_values], axis=2).astype(bf16)
    grad_projected = grad_projected.reshape(token_count, 3 * model_width)
    grad_qv_bias = jnp.stack(
        [
            jnp.sum(grad_projected[:, :model_width].astype(f32), axis=0),
            jnp.sum(grad_projected[:, 2 * model_width :].astype(f32), axis=0),
        ]
    )
    grad_qkv = jnp.einsum("td,te->de", normed_one, grad_projected, preferred_element_type=f32).astype(bf16)
    grad_normed_one = jnp.einsum("te,de->td", grad_projected, full_qkv, preferred_element_type=f32)
    grad_input_norm, grad_gain_one, grad_shift_one = norm_backward(
        grad_normed_one, unit_one, inverse_one, gain_one.astype(f32)
    )
    input_grad = (grad_hidden + grad_input_norm).reshape(batch_count, seq_length, model_width)
    bits = list(range(bits_of(size)))
    x_first = bits
    x_last = bits[:1] + bits[2:] + bits[1:2]
    sum_down = owner_sum(grad_down, x_first)
    sum_up = owner_sum(grad_up, x_last)
    sum_out = owner_sum(grad_out, x_first)
    half = grad_qkv.shape[1] // 2
    sum_qkv = jnp.concatenate(
        [owner_sum(grad_qkv[:, :half], x_first), owner_sum(grad_qkv[:, half:], x_last)], axis=1
    )
    small_grads = jnp.concatenate(
        [
            grad_qv_bias.reshape(2, size, -1).transpose(1, 0, 2).reshape(size, -1),
            by_owner(grad_out_bias),
            by_owner(grad_up_bias),
            by_owner(grad_down_bias),
            by_owner(grad_gain_one),
            by_owner(grad_shift_one),
            by_owner(grad_gain_two),
            by_owner(grad_shift_two),
            jnp.zeros((size, padding), f32),
        ],
        axis=1,
    )
    sum_small = replica_sum(halve(small_grads.reshape((2,) * len(bits) + (1, -1)), bits))[0]
    own = []
    offset = 0
    for width in widths:
        own.append(sum_small[offset : offset + width])
        offset += width
    return (
        encoded,
        input_grad,
        sum_qkv,
        own[0].reshape(2, -1),
        sum_out,
        own[1],
        sum_up,
        own[2],
        sum_down,
        own[3],
        own[4],
        own[5],
        own[6],
        own[7],
    )


def solution(mesh):
    in_specs = (
        P(("shard", "rep"), None, None),
        P(("shard", "rep")),
        P("shard", None),
        P(None, "shard"),
        P("shard", None),
        P("shard"),
        P("shard", None),
        P("shard"),
        P("shard", None),
        P("shard"),
        P("shard"),
        P("shard"),
        P("shard"),
        P("shard"),
        P(("shard", "rep"), None, None),
    )
    out_specs = (
        P(("shard", "rep"), None, None),
        P(("shard", "rep"), None, None),
        P("shard", None),
        P(None, "shard"),
        P("shard", None),
        P("shard"),
        P("shard", None),
        P("shard"),
        P("shard", None),
        P("shard"),
        P("shard"),
        P("shard"),
        P("shard"),
        P("shard"),
    )
    return jax.shard_map(shards, mesh=mesh, in_specs=in_specs, out_specs=out_specs, check_vma=False)
```

```python
import jax
import jax.numpy as jnp
from jax import lax
from jax.sharding import PartitionSpec as P

HEADS = 12
HEAD_DIM = 64


norm_eps = 1e-06


def normalize(value):
    average = jnp.mean(value, axis=-1, keepdims=True)
    centred = value - average
    variance = jnp.mean(centred * centred, axis=-1, keepdims=True)
    inverse = lax.rsqrt(variance + norm_eps)
    return (centred * inverse, inverse)


def norm_backward(grad_normed, unit_part, inverse, scales):
    grad_unit = grad_normed * scales
    mean_one = jnp.mean(grad_unit, axis=-1, keepdims=True)
    mean_two = jnp.mean(grad_unit * unit_part, axis=-1, keepdims=True)
    grad_input = inverse * (grad_unit - mean_one - unit_part * mean_two)
    return (grad_input, jnp.sum(grad_normed * unit_part, axis=0), jnp.sum(grad_normed, axis=0))


def exact_gelu(value):
    return jax.nn.gelu(value, approximate=False)


def bits_of(size):
    return size.bit_length() - 1


def swap(value, axis, bit):
    size = lax.axis_size(axis)
    return lax.ppermute(value, axis, [(i, i ^ (1 << bit)) for i in range(size)])


def halve(current, order):
    index = lax.axis_index("shard")
    remaining = list(range(bits_of(lax.axis_size("shard"))))[::-1]
    for bit in order:
        dim = remaining.index(bit)
        mine = (index >> bit) & 1
        sent = lax.dynamic_index_in_dim(current, 1 - mine, dim, keepdims=False)
        kept = lax.dynamic_index_in_dim(current, mine, dim, keepdims=False)
        came = swap(sent, "shard", bit)
        current = (kept.astype(jnp.float32) + came.astype(jnp.float32)).astype(current.dtype)
        remaining.remove(bit)
    return current


def gather_rows(own, order):
    index = lax.axis_index("shard")
    held = []
    current = own
    for bit in order:
        came = swap(current, "shard", bit)
        mine = ((index >> bit) & 1) == 0
        dim = len([other for other in held if other > bit])
        current = jnp.stack(
            [jnp.where(mine, current, came), jnp.where(mine, came, current)], axis=dim
        )
        held.append(bit)
    return current.reshape(-1, own.shape[-1])


def replica_sum(current):
    bits = bits_of(lax.axis_size("rep"))
    for bit in range(bits):
        came = swap(current, "rep", bit)
        total = current.astype(jnp.float32) + came.astype(jnp.float32)
        current = total.astype(current.dtype) if bit < bits - 1 else total
    return current.astype(jnp.float32)


def owner_sum(grad, order):
    size = lax.axis_size("shard")
    rows, columns = grad.shape
    split = grad.reshape((2,) * bits_of(size) + (rows // size, columns))
    return replica_sum(halve(split, order))


def by_owner(vector):
    return vector.reshape(lax.axis_size("shard"), -1)


def shards(
    images,
    image_counts,
    qkv_weight,
    qv_bias,
    out_weight,
    out_bias,
    up_weight,
    up_bias,
    down_weight,
    down_bias,
    norm1_gain,
    norm1_shift,
    norm2_gain,
    norm2_shift,
    cotangent,
):
    f32 = jnp.float32
    bf16 = jnp.bfloat16
    batch_count, seq_length, model_width = images.shape
    token_count = batch_count * seq_length
    score_scale = HEAD_DIM ** (-0.5)
    size = lax.axis_size("shard")
    small_parts = [
        qv_bias.reshape(-1),
        out_bias,
        up_bias,
        down_bias,
        norm1_gain,
        norm1_shift,
        norm2_gain,
        norm2_shift,
    ]
    widths = [part.shape[0] for part in small_parts]
    small_width = sum(widths)
    padding = -small_width % 128
    small_own = jnp.concatenate(small_parts + [jnp.zeros((padding,), bf16)])[None]
    outer_first = list(range(bits_of(size)))[::-1]
    small_full = gather_rows(small_own, outer_first)
    pieces = []
    offset = 0
    for width in widths:
        pieces.append(small_full[:, offset : offset + width])
        offset += width
    full_qv_bias = pieces[0].reshape(size, 2, -1).transpose(1, 0, 2).reshape(2, -1)
    (
        full_out_bias,
        full_up_bias,
        full_down_bias,
        gain_one,
        shift_one,
        gain_two,
        shift_two,
    ) = [piece.reshape(-1) for piece in pieces[1:]]
    full_qkv = gather_rows(qkv_weight, outer_first)
    full_out = gather_rows(out_weight, outer_first)
    full_up = gather_rows(up_weight, outer_first)
    full_down = gather_rows(down_weight, outer_first)
    live_mask = (jnp.arange(batch_count) < image_counts[0]).astype(f32)[:, None]
    live_rows = jnp.repeat(live_mask, seq_length, axis=0)
    inputs = images.astype(f32).reshape(token_count, model_width)
    unit_one, inverse_one = normalize(inputs)
    normed_one = (unit_one * gain_one.astype(f32) + shift_one.astype(f32)).astype(bf16)
    bias_row = jnp.concatenate(
        [full_qv_bias[0], jnp.zeros_like(full_qv_bias[0]), full_qv_bias[1]]
    ).astype(f32)
    projected = (jnp.dot(normed_one, full_qkv, preferred_element_type=f32) + bias_row).astype(bf16)
    projected = projected.reshape(batch_count, seq_length, 3, HEADS, HEAD_DIM)
    queries = projected[:, :, 0]
    keys_part = projected[:, :, 1]
    values = projected[:, :, 2]
    scores = (
        jnp.einsum("bqhd,bkhd->bhqk", queries, keys_part, preferred_element_type=f32) * score_scale
    )
    probs = jax.nn.softmax(scores, axis=-1)
    probs_low = probs.astype(bf16)
    attended = jnp.einsum("bhqk,bkhd->bqhd", probs_low, values, preferred_element_type=f32)
    attended = attended.reshape(token_count, model_width).astype(bf16)
    branch = jnp.dot(attended, full_out, preferred_element_type=f32) + full_out_bias.astype(f32)
    hidden = inputs + branch
    unit_two, inverse_two = normalize(hidden)
    normed_two = (unit_two * gain_two.astype(f32) + shift_two.astype(f32)).astype(bf16)
    upward = jnp.dot(normed_two, full_up, preferred_element_type=f32) + full_up_bias.astype(f32)
    activation, gelu_pull = jax.vjp(exact_gelu, upward)
    active_low = activation.astype(bf16)
    mlp_out = jnp.dot(active_low, full_down, preferred_element_type=f32) + full_down_bias.astype(
        f32
    )
    encoded = (
        ((hidden + mlp_out) * live_rows).astype(bf16).reshape(batch_count, seq_length, model_width)
    )
    grad_output = cotangent.astype(f32).reshape(token_count, model_width) * live_rows
    grad_mlp = grad_output.astype(bf16)
    grad_down_bias = jnp.sum(grad_mlp.astype(f32), axis=0)
    grad_down = jnp.einsum("tf,td->fd", active_low, grad_mlp, preferred_element_type=f32).astype(bf16)
    grad_active = jnp.einsum("td,fd->tf", grad_mlp, full_down, preferred_element_type=f32)
    grad_upward = gelu_pull(grad_active)[0].astype(bf16)
    grad_up_bias = jnp.sum(grad_upward.astype(f32), axis=0)
    grad_up = jnp.einsum("td,tf->df", normed_two, grad_upward, preferred_element_type=f32).astype(bf16)
    grad_normed_two = jnp.einsum("tf,df->td", grad_upward, full_up, preferred_element_type=f32)
    grad_hidden_norm, grad_gain_two, grad_shift_two = norm_backward(
        grad_normed_two, unit_two, inverse_two, gain_two.astype(f32)
    )
    grad_hidden = grad_output + grad_hidden_norm
    grad_branch = grad_hidden.astype(bf16)
    grad_out_bias = jnp.sum(grad_branch.astype(f32), axis=0)
    grad_out = jnp.einsum("td,te->de", attended, grad_branch, preferred_element_type=f32).astype(bf16)
    grad_attended = jnp.einsum(
        "te,de->td", grad_branch, full_out, preferred_element_type=f32
    ).astype(bf16)
    grad_attended = grad_attended.reshape(batch_count, seq_length, HEADS, HEAD_DIM)
    grad_probs = jnp.einsum("bqhd,bkhd->bhqk", grad_attended, values, preferred_element_type=f32)
    grad_values = jnp.einsum(
        "bhqk,bqhd->bkhd", probs_low, grad_attended, preferred_element_type=f32
    )
    row_terms = jnp.sum(probs * grad_probs, axis=-1, keepdims=True)
    grad_scores = (probs * (grad_probs - row_terms)).astype(bf16)
    grad_queries = (
        jnp.einsum("bhqk,bkhd->bqhd", grad_scores, keys_part, preferred_element_type=f32)
        * score_scale
    )
    grad_keys = (
        jnp.einsum("bhqk,bqhd->bkhd", grad_scores, queries, preferred_element_type=f32)
        * score_scale
    )
    grad_projected = jnp.stack([grad_queries, grad_keys, grad_values], axis=2).astype(bf16)
    grad_projected = grad_projected.reshape(token_count, 3 * model_width)
    grad_qv_bias = jnp.stack(
        [
            jnp.sum(grad_projected[:, :model_width].astype(f32), axis=0),
            jnp.sum(grad_projected[:, 2 * model_width :].astype(f32), axis=0),
        ]
    )
    grad_qkv = jnp.einsum("td,te->de", normed_one, grad_projected, preferred_element_type=f32).astype(bf16)
    grad_normed_one = jnp.einsum("te,de->td", grad_projected, full_qkv, preferred_element_type=f32)
    grad_input_norm, grad_gain_one, grad_shift_one = norm_backward(
        grad_normed_one, unit_one, inverse_one, gain_one.astype(f32)
    )
    input_grad = (grad_hidden + grad_input_norm).reshape(batch_count, seq_length, model_width)
    bits = list(range(bits_of(size)))
    x_first = bits
    x_last = bits[:1] + bits[2:] + bits[1:2]
    sum_down = owner_sum(grad_down, x_first)
    sum_up = owner_sum(grad_up, x_last)
    sum_out = owner_sum(grad_out, x_first)
    half = grad_qkv.shape[1] // 2
    sum_qkv = jnp.concatenate(
        [owner_sum(grad_qkv[:, :half], x_first), owner_sum(grad_qkv[:, half:], x_last)], axis=1
    )
    small_grads = jnp.concatenate(
        [
            grad_qv_bias.reshape(2, size, -1).transpose(1, 0, 2).reshape(size, -1),
            by_owner(grad_out_bias),
            by_owner(grad_up_bias),
            by_owner(grad_down_bias),
            by_owner(grad_gain_one),
            by_owner(grad_shift_one),
            by_owner(grad_gain_two),
            by_owner(grad_shift_two),
            jnp.zeros((size, padding), f32),
        ],
        axis=1,
    )
    sum_small = replica_sum(halve(small_grads.reshape((2,) * len(bits) + (1, -1)), bits))[0]
    own = []
    offset = 0
    for width in widths:
        own.append(sum_small[offset : offset + width])
        offset += width
    return (
        encoded,
        input_grad,
        sum_qkv,
        own[0].reshape(2, -1),
        sum_out,
        own[1],
        sum_up,
        own[2],
        sum_down,
        own[3],
        own[4],
        own[5],
        own[6],
        own[7],
    )


def solution(mesh):
    in_specs = (
        P(("shard", "rep"), None, None),
        P(("shard", "rep")),
        P("shard", None),
        P(None, "shard"),
        P("shard", None),
        P("shard"),
        P("shard", None),
        P("shard"),
        P("shard", None),
        P("shard"),
        P("shard"),
        P("shard"),
        P("shard"),
        P("shard"),
        P(("shard", "rep"), None, None),
    )
    out_specs = (
        P(("shard", "rep"), None, None),
        P(("shard", "rep"), None, None),
        P("shard", None),
        P(None, "shard"),
        P("shard", None),
        P("shard"),
        P("shard", None),
        P("shard"),
        P("shard", None),
        P("shard"),
        P("shard"),
        P("shard"),
        P("shard"),
        P("shard"),
    )
    return jax.shard_map(shards, mesh=mesh, in_specs=in_specs, out_specs=out_specs, check_vma=False)
```

```python
import jax
import jax.numpy as jnp
from jax import lax
from jax.sharding import PartitionSpec as P

HEADS = 12
HEAD_DIM = 64


norm_eps = 1e-06


def normalize(value):
    average = jnp.mean(value, axis=-1, keepdims=True)
    centred = value - average
    variance = jnp.mean(centred * centred, axis=-1, keepdims=True)
    inverse = lax.rsqrt(variance + norm_eps)
    return (centred * inverse, inverse)


def norm_backward(grad_normed, unit_part, inverse, scales):
    grad_unit = grad_normed * scales
    mean_one = jnp.mean(grad_unit, axis=-1, keepdims=True)
    mean_two = jnp.mean(grad_unit * unit_part, axis=-1, keepdims=True)
    grad_input = inverse * (grad_unit - mean_one - unit_part * mean_two)
    return (grad_input, jnp.sum(grad_normed * unit_part, axis=0), jnp.sum(grad_normed, axis=0))


def exact_gelu(value):
    return jax.nn.gelu(value, approximate=False)


def bits_of(size):
    return size.bit_length() - 1


def swap(value, axis, bit):
    size = lax.axis_size(axis)
    return lax.ppermute(value, axis, [(i, i ^ (1 << bit)) for i in range(size)])


def gather_step(current, bit, dim):
    mine = ((lax.axis_index("shard") >> bit) & 1) == 0
    came = swap(current, "shard", bit)
    return jnp.stack([jnp.where(mine, current, came), jnp.where(mine, came, current)], axis=dim)


def gather_from(current, order, done):
    for dim in range(done, len(order)):
        current = gather_step(current, order[dim], dim)
    return current.reshape(-1, current.shape[-1])


together = lax.optimization_barrier


class OwnerSum:
    def __init__(self, grad, order):
        size = lax.axis_size("shard")
        rows, columns = grad.shape
        self.current = grad.reshape((2,) * bits_of(size) + (rows // size, columns))
        self.remaining = list(range(bits_of(size)))[::-1]
        self.order = list(order)

    def step(self):
        bit = self.order.pop(0)
        index = lax.axis_index("shard")
        dim = self.remaining.index(bit)
        mine = (index >> bit) & 1
        sent = lax.dynamic_index_in_dim(self.current, 1 - mine, dim, keepdims=False)
        kept = lax.dynamic_index_in_dim(self.current, mine, dim, keepdims=False)
        came = swap(sent, "shard", bit)
        total = kept.astype(jnp.float32) + came.astype(jnp.float32)
        self.current = total.astype(self.current.dtype)
        self.remaining.remove(bit)

    def finish(self):
        while self.order:
            self.step()
        return replica_sum(self.current)


def replica_sum(current):
    bits = bits_of(lax.axis_size("rep"))
    for bit in range(bits):
        came = swap(current, "rep", bit)
        total = current.astype(jnp.float32) + came.astype(jnp.float32)
        current = total.astype(current.dtype) if bit < bits - 1 else total
    return current.astype(jnp.float32)


def by_owner(vector):
    return vector.reshape(lax.axis_size("shard"), -1)


def shards(
    images,
    image_counts,
    qkv_weight,
    qv_bias,
    out_weight,
    out_bias,
    up_weight,
    up_bias,
    down_weight,
    down_bias,
    norm1_gain,
    norm1_shift,
    norm2_gain,
    norm2_shift,
    cotangent,
):
    f32 = jnp.float32
    bf16 = jnp.bfloat16
    batch_count, seq_length, model_width = images.shape
    token_count = batch_count * seq_length
    score_scale = HEAD_DIM ** (-0.5)
    size = lax.axis_size("shard")
    small_parts = [
        qv_bias.reshape(-1),
        out_bias,
        up_bias,
        down_bias,
        norm1_gain,
        norm1_shift,
        norm2_gain,
        norm2_shift,
    ]
    widths = [part.shape[0] for part in small_parts]
    small_width = sum(widths)
    padding = -small_width % 128
    small_own = jnp.concatenate(small_parts + [jnp.zeros((padding,), bf16)])[None]
    outer_first = list(range(bits_of(size)))[::-1]
    small_full = gather_from(small_own, outer_first, 0)
    pieces = []
    offset = 0
    for width in widths:
        pieces.append(small_full[:, offset : offset + width])
        offset += width
    full_qv_bias = pieces[0].reshape(size, 2, -1).transpose(1, 0, 2).reshape(2, -1)
    (
        full_out_bias,
        full_up_bias,
        full_down_bias,
        gain_one,
        shift_one,
        gain_two,
        shift_two,
    ) = [piece.reshape(-1) for piece in pieces[1:]]
    inner = len(outer_first) - 2
    part_qkv = qkv_weight
    for dim in range(inner):
        part_qkv = gather_step(part_qkv, outer_first[dim], dim)
    full_qkv = gather_from(part_qkv, outer_first, inner)
    full_qkv, own_out, own_up, own_down = together((full_qkv, out_weight, up_weight, down_weight))
    part_out, part_up, part_down = [
        gather_step(own, outer_first[0], 0) for own in (own_out, own_up, own_down)
    ]
    live_mask = (jnp.arange(batch_count) < image_counts[0]).astype(f32)[:, None]
    live_rows = jnp.repeat(live_mask, seq_length, axis=0)
    inputs = images.astype(f32).reshape(token_count, model_width)
    unit_one, inverse_one = normalize(inputs)
    normed_one = (unit_one * gain_one.astype(f32) + shift_one.astype(f32)).astype(bf16)
    bias_row = jnp.concatenate(
        [full_qv_bias[0], jnp.zeros_like(full_qv_bias[0]), full_qv_bias[1]]
    ).astype(f32)
    projected = (jnp.dot(normed_one, full_qkv, preferred_element_type=f32) + bias_row).astype(bf16)
    projected = projected.reshape(batch_count, seq_length, 3, HEADS, HEAD_DIM)
    queries = projected[:, :, 0]
    keys_part = projected[:, :, 1]
    values = projected[:, :, 2]
    scores = (
        jnp.einsum("bqhd,bkhd->bhqk", queries, keys_part, preferred_element_type=f32) * score_scale
    )
    probs = jax.nn.softmax(scores, axis=-1)
    probs, part_out, part_up, part_down = together((probs, part_out, part_up, part_down))
    probs_low = probs.astype(bf16)
    part_out, part_up, part_down = [
        gather_step(part, outer_first[1], 1) for part in (part_out, part_up, part_down)
    ]
    attended = jnp.einsum("bhqk,bkhd->bqhd", probs_low, values, preferred_element_type=f32)
    attended = attended.reshape(token_count, model_width).astype(bf16)
    attended, part_out, part_up = together((attended, part_out, part_up))
    full_out = gather_from(part_out, outer_first, 2)
    full_up = gather_from(part_up, outer_first, 2)
    branch = jnp.dot(attended, full_out, preferred_element_type=f32) + full_out_bias.astype(f32)
    hidden = inputs + branch
    unit_two, inverse_two = normalize(hidden)
    normed_two = (unit_two * gain_two.astype(f32) + shift_two.astype(f32)).astype(bf16)
    normed_two, part_down = together((normed_two, part_down))
    for dim in range(2, len(outer_first) - 1):
        part_down = gather_step(part_down, outer_first[dim], dim)
    upward = jnp.dot(normed_two, full_up, preferred_element_type=f32) + full_up_bias.astype(f32)
    activation, gelu_pull = jax.vjp(exact_gelu, upward)
    active_low = activation.astype(bf16)
    active_low, part_down = together((active_low, part_down))
    full_down = gather_from(part_down, outer_first, len(outer_first) - 1)
    grad_output = cotangent.astype(f32).reshape(token_count, model_width) * live_rows
    grad_mlp = grad_output.astype(bf16)
    grad_down = jnp.einsum("tf,td->fd", active_low, grad_mlp, preferred_element_type=f32).astype(bf16)
    active_low, grad_down = together((active_low, grad_down))
    bits = list(range(bits_of(size)))
    x_first = bits
    x_last = bits[:1] + bits[2:] + bits[1:2]
    down_sum = OwnerSum(grad_down, x_first)
    down_sum.step()
    mlp_out = jnp.dot(active_low, full_down, preferred_element_type=f32) + full_down_bias.astype(
        f32
    )
    encoded = (
        ((hidden + mlp_out) * live_rows).astype(bf16).reshape(batch_count, seq_length, model_width)
    )
    grad_down_bias = jnp.sum(grad_mlp.astype(f32), axis=0)
    grad_active = jnp.einsum("td,fd->tf", grad_mlp, full_down, preferred_element_type=f32)
    grad_upward = gelu_pull(grad_active)[0].astype(bf16)
    grad_up_bias = jnp.sum(grad_upward.astype(f32), axis=0)
    grad_up = jnp.einsum("td,tf->df", normed_two, grad_upward, preferred_element_type=f32).astype(bf16)
    grad_upward, grad_up, down_sum.current = together((grad_upward, grad_up, down_sum.current))
    down_sum.step()
    up_sum = OwnerSum(grad_up, x_last)
    up_sum.step()
    grad_normed_two = jnp.einsum("tf,df->td", grad_upward, full_up, preferred_element_type=f32)
    grad_hidden_norm, grad_gain_two, grad_shift_two = norm_backward(
        grad_normed_two, unit_two, inverse_two, gain_two.astype(f32)
    )
    grad_hidden = grad_output + grad_hidden_norm
    grad_branch = grad_hidden.astype(bf16)
    grad_out_bias = jnp.sum(grad_branch.astype(f32), axis=0)
    grad_out = jnp.einsum("td,te->de", attended, grad_branch, preferred_element_type=f32).astype(bf16)
    grad_branch, grad_out, up_sum.current = together((grad_branch, grad_out, up_sum.current))
    up_sum.step()
    out_sum = OwnerSum(grad_out, x_first)
    out_sum.step()
    grad_attended = jnp.einsum(
        "te,de->td", grad_branch, full_out, preferred_element_type=f32
    ).astype(bf16)
    grad_attended = grad_attended.reshape(batch_count, seq_length, HEADS, HEAD_DIM)
    grad_probs = jnp.einsum("bqhd,bkhd->bhqk", grad_attended, values, preferred_element_type=f32)
    grad_values = jnp.einsum(
        "bhqk,bqhd->bkhd", probs_low, grad_attended, preferred_element_type=f32
    )
    grad_probs, down_sum.current, out_sum.current = together(
        (grad_probs, down_sum.current, out_sum.current)
    )
    down_sum.step()
    row_terms = jnp.sum(probs * grad_probs, axis=-1, keepdims=True)
    grad_scores = (probs * (grad_probs - row_terms)).astype(bf16)
    grad_scores, down_sum.current, up_sum.current = together(
        (grad_scores, down_sum.current, up_sum.current)
    )
    down_sum.step()
    up_sum.step()
    grad_queries = (
        jnp.einsum("bhqk,bkhd->bqhd", grad_scores, keys_part, preferred_element_type=f32)
        * score_scale
    )
    grad_keys = (
        jnp.einsum("bhqk,bqhd->bkhd", grad_scores, queries, preferred_element_type=f32)
        * score_scale
    )
    grad_projected = jnp.stack([grad_queries, grad_keys, grad_values], axis=2).astype(bf16)
    grad_projected = grad_projected.reshape(token_count, 3 * model_width)
    grad_qv_bias = jnp.stack(
        [
            jnp.sum(grad_projected[:, :model_width].astype(f32), axis=0),
            jnp.sum(grad_projected[:, 2 * model_width :].astype(f32), axis=0),
        ]
    )
    grad_qkv = jnp.einsum("td,te->de", normed_one, grad_projected, preferred_element_type=f32).astype(bf16)
    grad_normed_one = jnp.einsum("te,de->td", grad_projected, full_qkv, preferred_element_type=f32)
    grad_input_norm, grad_gain_one, grad_shift_one = norm_backward(
        grad_normed_one, unit_one, inverse_one, gain_one.astype(f32)
    )
    input_grad = (grad_hidden + grad_input_norm).reshape(batch_count, seq_length, model_width)
    half = grad_qkv.shape[1] // 2
    sum_qkv = jnp.concatenate(
        [
            OwnerSum(grad_qkv[:, :half], x_first).finish(),
            OwnerSum(grad_qkv[:, half:], x_last).finish(),
        ],
        axis=1,
    )
    sum_down = down_sum.finish()
    sum_up = up_sum.finish()
    sum_out = out_sum.finish()
    small_grads = jnp.concatenate(
        [
            grad_qv_bias.reshape(2, size, -1).transpose(1, 0, 2).reshape(size, -1),
            by_owner(grad_out_bias),
            by_owner(grad_up_bias),
            by_owner(grad_down_bias),
            by_owner(grad_gain_one),
            by_owner(grad_shift_one),
            by_owner(grad_gain_two),
            by_owner(grad_shift_two),
            jnp.zeros((size, padding), f32),
        ],
        axis=1,
    )
    sum_small = OwnerSum(small_grads, bits).finish()[0]
    own = []
    offset = 0
    for width in widths:
        own.append(sum_small[offset : offset + width])
        offset += width
    return (
        encoded,
        input_grad,
        sum_qkv,
        own[0].reshape(2, -1),
        sum_out,
        own[1],
        sum_up,
        own[2],
        sum_down,
        own[3],
        own[4],
        own[5],
        own[6],
        own[7],
    )


def solution(mesh):
    in_specs = (
        P(("shard", "rep"), None, None),
        P(("shard", "rep")),
        P("shard", None),
        P(None, "shard"),
        P("shard", None),
        P("shard"),
        P("shard", None),
        P("shard"),
        P("shard", None),
        P("shard"),
        P("shard"),
        P("shard"),
        P("shard"),
        P("shard"),
        P(("shard", "rep"), None, None),
    )
    out_specs = (
        P(("shard", "rep"), None, None),
        P(("shard", "rep"), None, None),
        P("shard", None),
        P(None, "shard"),
        P("shard", None),
        P("shard"),
        P("shard", None),
        P("shard"),
        P("shard", None),
        P("shard"),
        P("shard"),
        P("shard"),
        P("shard"),
        P("shard"),
    )
    return jax.shard_map(shards, mesh=mesh, in_specs=in_specs, out_specs=out_specs, check_vma=False)
```

```python
import jax
import jax.numpy as jnp
from jax import lax
from jax.sharding import PartitionSpec as P

HEADS = 12
HEAD_DIM = 64


norm_eps = 1e-06


def normalize(value):
    average = jnp.mean(value, axis=-1, keepdims=True)
    centred = value - average
    variance = jnp.mean(centred * centred, axis=-1, keepdims=True)
    inverse = lax.rsqrt(variance + norm_eps)
    return (centred * inverse, inverse)


def norm_backward(grad_normed, unit_part, inverse, scales):
    grad_unit = grad_normed * scales
    mean_one = jnp.mean(grad_unit, axis=-1, keepdims=True)
    mean_two = jnp.mean(grad_unit * unit_part, axis=-1, keepdims=True)
    grad_input = inverse * (grad_unit - mean_one - unit_part * mean_two)
    return (grad_input, jnp.sum(grad_normed * unit_part, axis=0), jnp.sum(grad_normed, axis=0))


def exact_gelu(value):
    return jax.nn.gelu(value, approximate=False)


def bits_of(size):
    return size.bit_length() - 1


def swap(value, axis, bit):
    size = lax.axis_size(axis)
    return lax.ppermute(value, axis, [(i, i ^ (1 << bit)) for i in range(size)])


def gather_step(current, bit, dim):
    mine = ((lax.axis_index("shard") >> bit) & 1) == 0
    came = swap(current, "shard", bit)
    return jnp.stack([jnp.where(mine, current, came), jnp.where(mine, came, current)], axis=dim)


def gather_from(current, order, done):
    for dim in range(done, len(order)):
        current = gather_step(current, order[dim], dim)
    return current.reshape(-1, current.shape[-1])


together = lax.optimization_barrier


class OwnerSum:
    def __init__(self, grad, order):
        size = lax.axis_size("shard")
        rows, columns = grad.shape
        self.current = grad.reshape((2,) * bits_of(size) + (rows // size, columns))
        self.remaining = list(range(bits_of(size)))[::-1]
        self.order = list(order)

    def step(self):
        bit = self.order.pop(0)
        index = lax.axis_index("shard")
        dim = self.remaining.index(bit)
        mine = (index >> bit) & 1
        sent = lax.dynamic_index_in_dim(self.current, 1 - mine, dim, keepdims=False)
        kept = lax.dynamic_index_in_dim(self.current, mine, dim, keepdims=False)
        came = swap(sent, "shard", bit)
        total = kept.astype(jnp.float32) + came.astype(jnp.float32)
        self.current = total.astype(self.current.dtype)
        self.remaining.remove(bit)

    def finish(self):
        while self.order:
            self.step()
        return replica_sum(self.current)


def replica_sum(current):
    bits = bits_of(lax.axis_size("rep"))
    for bit in range(bits):
        came = swap(current, "rep", bit)
        total = current.astype(jnp.float32) + came.astype(jnp.float32)
        current = total.astype(current.dtype) if bit < bits - 1 else total
    return current.astype(jnp.float32)


def by_owner(vector):
    return vector.reshape(lax.axis_size("shard"), -1)


def shards(
    images,
    image_counts,
    qkv_weight,
    qv_bias,
    out_weight,
    out_bias,
    up_weight,
    up_bias,
    down_weight,
    down_bias,
    norm1_gain,
    norm1_shift,
    norm2_gain,
    norm2_shift,
    cotangent,
):
    f32 = jnp.float32
    bf16 = jnp.bfloat16
    batch_count, seq_length, model_width = images.shape
    token_count = batch_count * seq_length
    score_scale = HEAD_DIM ** (-0.5)
    size = lax.axis_size("shard")
    small_parts = [
        qv_bias.reshape(-1),
        out_bias,
        up_bias,
        down_bias,
        norm1_gain,
        norm1_shift,
        norm2_gain,
        norm2_shift,
    ]
    widths = [part.shape[0] for part in small_parts]
    small_width = sum(widths)
    padding = -small_width % 128
    small_own = jnp.concatenate(small_parts + [jnp.zeros((padding,), bf16)])[None]
    outer_first = list(range(bits_of(size)))[::-1]
    small_full = gather_from(small_own, outer_first, 0)
    pieces = []
    offset = 0
    for width in widths:
        pieces.append(small_full[:, offset : offset + width])
        offset += width
    full_qv_bias = pieces[0].reshape(size, 2, -1).transpose(1, 0, 2).reshape(2, -1)
    (
        full_out_bias,
        full_up_bias,
        full_down_bias,
        gain_one,
        shift_one,
        gain_two,
        shift_two,
    ) = [piece.reshape(-1) for piece in pieces[1:]]
    last = len(outer_first) - 1
    full_qkv = gather_from(qkv_weight, outer_first, 0)
    full_out = gather_from(out_weight, outer_first, 0)
    part_up, part_down = up_weight, down_weight
    for dim in range(last - 1):
        part_up = gather_step(part_up, outer_first[dim], dim)
        part_down = gather_step(part_down, outer_first[dim], dim)
    full_qkv, part_up, part_down = together((full_qkv, part_up, part_down))
    part_up = gather_step(part_up, outer_first[last - 1], last - 1)
    part_down = gather_step(part_down, outer_first[last - 1], last - 1)
    live_mask = (jnp.arange(batch_count) < image_counts[0]).astype(f32)[:, None]
    live_rows = jnp.repeat(live_mask, seq_length, axis=0)
    inputs = images.astype(f32).reshape(token_count, model_width)
    unit_one, inverse_one = normalize(inputs)
    normed_one = (unit_one * gain_one.astype(f32) + shift_one.astype(f32)).astype(bf16)
    bias_row = jnp.concatenate(
        [full_qv_bias[0], jnp.zeros_like(full_qv_bias[0]), full_qv_bias[1]]
    ).astype(f32)
    projected = (jnp.dot(normed_one, full_qkv, preferred_element_type=f32) + bias_row).astype(bf16)
    projected = projected.reshape(batch_count, seq_length, 3, HEADS, HEAD_DIM)
    queries = projected[:, :, 0]
    keys_part = projected[:, :, 1]
    values = projected[:, :, 2]
    scores = (
        jnp.einsum("bqhd,bkhd->bhqk", queries, keys_part, preferred_element_type=f32) * score_scale
    )
    probs = jax.nn.softmax(scores, axis=-1)
    probs_low = probs.astype(bf16)
    attended = jnp.einsum("bhqk,bkhd->bqhd", probs_low, values, preferred_element_type=f32)
    attended = attended.reshape(token_count, model_width).astype(bf16)
    attended, part_up, part_down = together((attended, part_up, part_down))
    full_up = gather_from(part_up, outer_first, last)
    full_down = gather_from(part_down, outer_first, last)
    branch = jnp.dot(attended, full_out, preferred_element_type=f32) + full_out_bias.astype(f32)
    hidden = inputs + branch
    unit_two, inverse_two = normalize(hidden)
    normed_two = (unit_two * gain_two.astype(f32) + shift_two.astype(f32)).astype(bf16)
    upward = jnp.dot(normed_two, full_up, preferred_element_type=f32) + full_up_bias.astype(f32)
    activation, gelu_pull = jax.vjp(exact_gelu, upward)
    active_low = activation.astype(bf16)
    grad_output = cotangent.astype(f32).reshape(token_count, model_width) * live_rows
    grad_mlp = grad_output.astype(bf16)
    grad_down = jnp.einsum("tf,td->fd", active_low, grad_mlp, preferred_element_type=f32).astype(bf16)
    active_low, grad_down = together((active_low, grad_down))
    bits = list(range(bits_of(size)))
    x_first = bits
    x_last = bits[:1] + bits[2:] + bits[1:2]
    down_sum = OwnerSum(grad_down, x_first)
    down_sum.step()
    mlp_out = jnp.dot(active_low, full_down, preferred_element_type=f32) + full_down_bias.astype(
        f32
    )
    encoded = (
        ((hidden + mlp_out) * live_rows).astype(bf16).reshape(batch_count, seq_length, model_width)
    )
    grad_down_bias = jnp.sum(grad_mlp.astype(f32), axis=0)
    grad_active = jnp.einsum("td,fd->tf", grad_mlp, full_down, preferred_element_type=f32)
    grad_upward = gelu_pull(grad_active)[0].astype(bf16)
    grad_up_bias = jnp.sum(grad_upward.astype(f32), axis=0)
    grad_up = jnp.einsum("td,tf->df", normed_two, grad_upward, preferred_element_type=f32).astype(bf16)
    grad_upward, grad_up, down_sum.current = together((grad_upward, grad_up, down_sum.current))
    down_sum.step()
    up_sum = OwnerSum(grad_up, x_last)
    up_sum.step()
    grad_normed_two = jnp.einsum("tf,df->td", grad_upward, full_up, preferred_element_type=f32)
    grad_hidden_norm, grad_gain_two, grad_shift_two = norm_backward(
        grad_normed_two, unit_two, inverse_two, gain_two.astype(f32)
    )
    grad_hidden = grad_output + grad_hidden_norm
    grad_branch = grad_hidden.astype(bf16)
    grad_out_bias = jnp.sum(grad_branch.astype(f32), axis=0)
    grad_out = jnp.einsum("td,te->de", attended, grad_branch, preferred_element_type=f32).astype(bf16)
    grad_branch, grad_out, up_sum.current = together((grad_branch, grad_out, up_sum.current))
    up_sum.step()
    out_sum = OwnerSum(grad_out, x_first)
    out_sum.step()
    grad_attended = jnp.einsum(
        "te,de->td", grad_branch, full_out, preferred_element_type=f32
    ).astype(bf16)
    grad_attended = grad_attended.reshape(batch_count, seq_length, HEADS, HEAD_DIM)
    grad_probs = jnp.einsum("bqhd,bkhd->bhqk", grad_attended, values, preferred_element_type=f32)
    grad_values = jnp.einsum(
        "bhqk,bqhd->bkhd", probs_low, grad_attended, preferred_element_type=f32
    )
    row_terms = jnp.sum(probs * grad_probs, axis=-1, keepdims=True)
    grad_scores = (probs * (grad_probs - row_terms)).astype(bf16)
    grad_scores, down_sum.current, up_sum.current = together(
        (grad_scores, down_sum.current, up_sum.current)
    )
    down_sum.step()
    up_sum.step()
    grad_queries = (
        jnp.einsum("bhqk,bkhd->bqhd", grad_scores, keys_part, preferred_element_type=f32)
        * score_scale
    )
    grad_keys = (
        jnp.einsum("bhqk,bqhd->bkhd", grad_scores, queries, preferred_element_type=f32)
        * score_scale
    )
    grad_projected = jnp.stack([grad_queries, grad_keys, grad_values], axis=2).astype(bf16)
    grad_projected = grad_projected.reshape(token_count, 3 * model_width)
    grad_projected, out_sum.current = together((grad_projected, out_sum.current))
    grad_qv_bias = jnp.stack(
        [
            jnp.sum(grad_projected[:, :model_width].astype(f32), axis=0),
            jnp.sum(grad_projected[:, 2 * model_width :].astype(f32), axis=0),
        ]
    )
    grad_qkv = jnp.einsum("td,te->de", normed_one, grad_projected, preferred_element_type=f32).astype(bf16)
    grad_normed_one = jnp.einsum("te,de->td", grad_projected, full_qkv, preferred_element_type=f32)
    grad_input_norm, grad_gain_one, grad_shift_one = norm_backward(
        grad_normed_one, unit_one, inverse_one, gain_one.astype(f32)
    )
    input_grad = (grad_hidden + grad_input_norm).reshape(batch_count, seq_length, model_width)
    half = grad_qkv.shape[1] // 2
    left_sum = OwnerSum(grad_qkv[:, :half], x_first)
    left_sum.step()
    right_sum = OwnerSum(grad_qkv[:, half:], x_last)
    right_sum.step()
    sum_down = down_sum.finish()
    sum_up = up_sum.finish()
    sum_out = out_sum.finish()
    small_grads = jnp.concatenate(
        [
            grad_qv_bias.reshape(2, size, -1).transpose(1, 0, 2).reshape(size, -1),
            by_owner(grad_out_bias),
            by_owner(grad_up_bias),
            by_owner(grad_down_bias),
            by_owner(grad_gain_one),
            by_owner(grad_shift_one),
            by_owner(grad_gain_two),
            by_owner(grad_shift_two),
            jnp.zeros((size, padding), f32),
        ],
        axis=1,
    )
    small_grads, left_sum.current, right_sum.current = together(
        (small_grads, left_sum.current, right_sum.current)
    )
    sum_qkv = jnp.concatenate([left_sum.finish(), right_sum.finish()], axis=1)
    sum_small = OwnerSum(small_grads, bits).finish()[0]
    own = []
    offset = 0
    for width in widths:
        own.append(sum_small[offset : offset + width])
        offset += width
    return (
        encoded,
        input_grad,
        sum_qkv,
        own[0].reshape(2, -1),
        sum_out,
        own[1],
        sum_up,
        own[2],
        sum_down,
        own[3],
        own[4],
        own[5],
        own[6],
        own[7],
    )


def solution(mesh):
    in_specs = (
        P(("shard", "rep"), None, None),
        P(("shard", "rep")),
        P("shard", None),
        P(None, "shard"),
        P("shard", None),
        P("shard"),
        P("shard", None),
        P("shard"),
        P("shard", None),
        P("shard"),
        P("shard"),
        P("shard"),
        P("shard"),
        P("shard"),
        P(("shard", "rep"), None, None),
    )
    out_specs = (
        P(("shard", "rep"), None, None),
        P(("shard", "rep"), None, None),
        P("shard", None),
        P(None, "shard"),
        P("shard", None),
        P("shard"),
        P("shard", None),
        P("shard"),
        P("shard", None),
        P("shard"),
        P("shard"),
        P("shard"),
        P("shard"),
        P("shard"),
    )
    return jax.shard_map(shards, mesh=mesh, in_specs=in_specs, out_specs=out_specs, check_vma=False)
```
